256 devices in a mesh: blk: 256 (over z, x, y, core).
Axes of the slice: x: 4, y: 4, z: 8, core: 2. Of those that a mesh axis runs over, the one named last changes fastest.
Arguments:
- adjacency: int32 [65536, 1280], P('blk'), may hold values 0 or 1
- weight: bfloat16 [65536, 1280], P('blk'), may hold values from -6 to 6
Outputs:
- closure: float32 [65536, 4352], P('blk')
The draws below stay inside these ranges and needn't reach their ends.
All inputs are finite; a program needn't handle non-finite values. No bound on the sum of `adjacency` on one device may be relied on, other than what follows from the above.
Results may differ from the reference program's by a relative error of at most 0.0041.
Values may be sent and summed in bfloat16 or wider, within the bound.
No kernel may reach another device: no remote copies, remote signals or barrier semaphores. Data moves between devices by JAX's collectives and lax.ppermute only.
A program may use at most 64 MiB of HBM per device.

```python
import math
import jax
import jax.numpy as jnp
from jax import lax

B = 512
R = 256
K = 2
N = 65536


def place_ends(array, stream_key, least, largest):
    index_at = [jax.random.randint(jax.random.fold_in(stream_key, axis), (), 0, length) for axis, length in enumerate(array.shape)]
    main_axis = array.shape.index(max(array.shape))
    next_to = index_at[:main_axis] + [(index_at[main_axis] + 1) % array.shape[main_axis]] + index_at[main_axis + 1:]
    return array.at[tuple(index_at)].set(least).at[tuple(next_to)].set(largest)


def block_levels(own_key, shape, cuts, smallest, high):
    def one(dim, blocks):
        steps = jax.random.uniform(jax.random.fold_in(jax.random.fold_in(own_key, 6), dim), (blocks,), jnp.float32, smallest / len(cuts), high / len(cuts))
        return jnp.repeat(jnp.exp(steps), shape[dim] // blocks).reshape((-1,) + (1,) * (len(shape) - dim - 1))

    factor_of = one(*cuts[0])
    for cut in cuts[1:]:
        factor_of = factor_of * one(*cut)
    return factor_of


def noise(own_key, shape, scale, most, pieces=(), dtype=jnp.bfloat16):
    values = jax.random.normal(own_key, shape, jnp.float32) * scale
    if len(pieces) > 0:
        values = block_levels(own_key, shape, pieces, -0.22, 0.18) * values
    return jnp.clip(values, min=-most, max=most).astype(dtype)


def setup_inputs(seed: int = 0) -> dict:
    streams_of = jax.random.split(jax.random.key(seed), 3)
    return {
        "adjacency": place_ends((jax.random.randint(streams_of[0], (N, (2 * K + 1) * R), 0, 2) < 1).astype(jnp.int32), jax.random.fold_in(streams_of[0], 1), 0, 1),
        "weight": noise(streams_of[1], (N, (2 * K + 1) * R), 1.0, 6.0, ((0, 256),)),
    }


def banded(adjacency, weight):
    reach = (adjacency.shape[1] // R - 1) // 2
    local_row = lax.broadcasted_iota(jnp.int32, adjacency.shape, 0) % R
    offset = lax.broadcasted_iota(jnp.int32, adjacency.shape, 1) - local_row - reach * R
    keep = (jnp.abs(offset) <= B) & ((adjacency == 1) | (offset == 0))
    return jnp.where(keep, weight, jnp.zeros_like(weight))

def square(matrix, scale):
    block_count = matrix.shape[0] // R
    width_cols = matrix.shape[1]
    reach = (width_cols // R - 1) // 2
    blocks = matrix.reshape(block_count, R, width_cols)
    result = jnp.zeros((block_count, R, (4 * reach + 1) * R), jnp.float32)
    for column in range(2 * reach + 1):
        neighbour = jnp.roll(blocks, -(column - reach), axis=0).astype(jnp.float32)
        left = blocks[:, :, column * R:(column + 1) * R].astype(jnp.float32)
        product = jnp.einsum('bij,bjk->bik', left, neighbour)
        result = result.at[:, :, column * R:column * R + width_cols].add(product)
    return (result * scale).reshape(block_count * R, (4 * reach + 1) * R)

def reference(adjacency, weight):
    matrix = banded(adjacency, weight)
    first = square(matrix, 1.0 / math.sqrt(B)).astype(jnp.bfloat16)
    return square(first, 1.0 / math.sqrt(2 * B))
```

```python
import math

import jax
import jax.numpy as jnp
from jax import lax
from jax.experimental import pallas as pl
from jax.experimental.pallas import tpu as pltpu
from jax.sharding import PartitionSpec as P

B = 512
R = 256
LANES = 128
TILES = 1024 // LANES
ROWS = TILES * R + 16
FIRST_SCALE = 1.0 / math.sqrt(B)
LAST_SCALE = 1.0 / (math.sqrt(B) * math.sqrt(2 * B))
MIB = 1 << 20


def pack_kernel(adjacency_ref, weight_ref, packed_ref, far_ref):
    step = pl.program_id(0)
    count = adjacency_ref.shape[0]
    row = lax.broadcasted_iota(jnp.int32, (count, LANES), 0) + step * count
    lane = lax.broadcasted_iota(jnp.int32, (count, LANES), 1)

    def tile(index):
        columns = slice(index * LANES, (index + 1) * LANES)
        edge = adjacency_ref[:, columns] == 1
        value = weight_ref[:, columns].astype(jnp.float32)
        return edge, value

    for half in range(2):
        column = lane + half * LANES
        near_edge, near = tile(half)
        far_edge, far = tile(8 + half)
        near = jnp.where(near_edge, near, 0.0)
        far = jnp.where(far_edge, far, 0.0)
        merged = jnp.where(column >= row, near, far)
        packed_ref[pl.ds(half * R + step * count, count), :] = merged.astype(jnp.bfloat16)
        diagonal = jnp.sum(jnp.where(column == row, far, 0.0), axis=0, keepdims=True)
        previous = jnp.where(step == 0, 0.0, far_ref[half : half + 1, :])
        far_ref[half : half + 1, :] = previous + diagonal
    for index in range(2, 8):
        edge, value = tile(index)
        if index in (4, 5):
            edge = edge | (lane + (index - 4) * LANES == row)
        kept = jnp.where(edge, value, 0.0)
        packed_ref[pl.ds(index * R + step * count, count), :] = kept.astype(jnp.bfloat16)

    @pl.when(step == pl.num_programs(0) - 1)
    def _():
        place = lax.broadcasted_iota(jnp.int32, (16, LANES), 0)
        first = jnp.where(place == 0, far_ref[0:1, :], 0.0)
        both = first + jnp.where(place == 1, far_ref[1:2, :], 0.0)
        packed_ref[TILES * R :, :] = both.astype(jnp.bfloat16)


def pack(adjacency, weight):
    steps = 4
    return pl.pallas_call(
        pack_kernel,
        grid=(steps,),
        in_specs=[pl.BlockSpec((R // steps, 5 * R), lambda i: (i, 0))] * 2,
        out_specs=pl.BlockSpec((ROWS, LANES), lambda i: (0, 0)),
        out_shape=jax.ShapeDtypeStruct((ROWS, LANES), jnp.bfloat16),
        scratch_shapes=[pltpu.VMEM((8, LANES), jnp.float32)],
        compiler_params=pltpu.CompilerParams(vmem_limit_bytes=16 * MIB),
        cost_estimate=pl.CostEstimate(flops=R * 5 * R * 4, bytes_accessed=R * 5 * R * 6 + ROWS * 256, transcendentals=0),
    )(adjacency, weight)


def slot(ref, index):
    begin = index * 2 * R
    return jnp.concatenate([ref[begin : begin + R, :], ref[begin + R : begin + 2 * R, :]], axis=1)


def unpacked(ref):
    row = lax.broadcasted_iota(jnp.int32, (R, R), 0)
    column = lax.broadcasted_iota(jnp.int32, (R, R), 1)
    merged = slot(ref, 0).astype(jnp.float32)
    tail = ref[TILES * R :, :].astype(jnp.float32)
    diagonal = jnp.concatenate([tail[0:1, :], tail[1:2, :]], axis=1)
    first = jnp.where(column >= row, merged, 0.0)
    last = jnp.where(column < row, merged, jnp.where(column == row, diagonal, 0.0))
    return [
        first.astype(jnp.bfloat16),
        slot(ref, 1),
        slot(ref, 2),
        slot(ref, 3),
        last.astype(jnp.bfloat16),
    ]


def block(index):
    return pl.ds(pl.multiple_of(index * R, R), R)


def accumulate(total_ref, left, ref, first_block):
    for offset, right in enumerate(unpacked(ref)):
        where = block(first_block + offset)
        total_ref[:, where] += jnp.dot(left, right, preferred_element_type=jnp.float32)


def square_kernel(sign_ref, own, n1, p1, n2, p2, result_ref, left_ref, total_ref):
    sign = sign_ref[0]
    for offset, part in enumerate(unpacked(own)):
        left_ref[:, offset * R : (offset + 1) * R] = part
    total_ref[...] = jnp.zeros_like(total_ref)
    for reach, ref in ((0, own), (1, p1), (-1, n1), (2, p2), (-2, n2)):
        at = reach * sign
        accumulate(total_ref, left_ref[:, block(at + 2)], ref, at + 2)
    result_ref[...] = (total_ref[...] * FIRST_SCALE).astype(jnp.bfloat16)


def cube_kernel(sign_ref, left_ref, d0, n1, p1, n2, p2, n3, p3, n4, p4, cube_ref, sum_ref, total_ref):
    sign = sign_ref[0]
    known = ((0, d0), (1, p1), (-1, n1), (2, p2), (-2, n2), (3, p3), (-3, n3), (4, p4), (-4, n4))
    total_ref[...] = jnp.zeros_like(total_ref)
    for reach, ref in known:
        at = reach * sign
        accumulate(total_ref, left_ref[:, block(at + 4)], ref, at + 4)
    cube_ref[...] = total_ref[...].astype(jnp.bfloat16)
    sum_ref[...] = jnp.zeros_like(sum_ref)
    for reach, ref in known:
        at = reach * sign
        accumulate(sum_ref, cube_ref[:, block(at + 6)], ref, at + 4)


def far_kernel(sign_ref, cube_ref, sum_ref, n5, p5, p6, out_ref, last_ref):
    sign = sign_ref[0]
    out_ref[:, : 2 * R] = jnp.zeros((R, 2 * R), jnp.float32)
    out_ref[:, 15 * R :] = jnp.zeros((R, 2 * R), jnp.float32)
    out_ref[:, 2 * R : 15 * R] = sum_ref[...]
    for reach, ref in ((5, p5), (-5, n5), (6, p6)):
        at = reach * sign
        accumulate(out_ref, cube_ref[:, block(at + 6)], ref, at + 6)
    out_ref[...] = out_ref[...] * LAST_SCALE
    last_ref[...] = cube_ref[:, block(6 - 6 * sign)]


def edge_kernel(left_ref, n6, before_ref, out_ref):
    step = pl.program_id(0)
    for offset, right in enumerate(unpacked(n6)):

        @pl.when(step == offset)
        def _():
            product = jnp.dot(left_ref[...], right, preferred_element_type=jnp.float32)
            out_ref[...] = before_ref[...] + product * LAST_SCALE


def edge_call(sign, left, n6, before):
    def place(i, sign_ref):
        return (0, 6 - 6 * sign_ref[0] + i)

    def kernel(sign_ref, *refs):
        edge_kernel(*refs)

    return pl.pallas_call(
        kernel,
        grid_spec=pltpu.PrefetchScalarGridSpec(
            num_scalar_prefetch=1,
            grid=(5,),
            in_specs=[
                pl.BlockSpec((R, R), lambda i, s: (0, 0)),
                pl.BlockSpec((ROWS, LANES), lambda i, s: (0, 0)),
                pl.BlockSpec((R, R), place),
            ],
            out_specs=pl.BlockSpec((R, R), place),
        ),
        out_shape=jax.ShapeDtypeStruct(before.shape, jnp.float32),
        input_output_aliases={3: 0},
        compiler_params=pltpu.CompilerParams(vmem_limit_bytes=16 * MIB),
        cost_estimate=cost(1, 2 * 5 * R * R * 4),
    )(sign, left, n6, before)


def cost(count, more):
    return pl.CostEstimate(
        flops=count * 2 * R * R * 5 * R, bytes_accessed=count * ROWS * LANES * 2 + more, transcendentals=0
    )


def call(kernel, arrays, shapes, scratch, count, more):
    specs = [pl.BlockSpec(memory_space=pltpu.SMEM)]
    specs += [pl.BlockSpec(memory_space=pltpu.VMEM)] * (len(arrays) - 1)
    return pl.pallas_call(
        kernel,
        in_specs=specs,
        out_specs=[pl.BlockSpec(memory_space=pltpu.VMEM)] * len(shapes),
        out_shape=shapes,
        scratch_shapes=scratch,
        compiler_params=pltpu.CompilerParams(vmem_limit_bytes=40 * MIB),
        cost_estimate=cost(count, more),
    )(*arrays)


def local(adjacency, weight):
    size = lax.axis_size("blk")
    parity = lax.rem(lax.axis_index("blk"), 2)
    sign = (1 - 2 * parity).astype(jnp.int32).reshape(1)

    def hop(value, steps):
        pairs = []
        for target in range(size):
            ahead = steps if target % 2 == 0 else -steps
            pairs.append(((target + ahead) % size, target))
        return lax.ppermute(value, "blk", pairs)

    def peer(value):
        return lax.ppermute(value, "blk", [(source, source ^ 1) for source in range(size)])

    own = pack(adjacency, weight)
    p2 = hop(own, 2)
    p1 = peer(own)
    held, p1 = lax.optimization_barrier((own, p1))
    n2 = hop(held, -2)
    p4 = hop(p2, 2)
    n1 = peer(p2)
    n4 = hop(n2, -2)
    p3 = peer(n2)
    f32, bf16 = jnp.float32, jnp.bfloat16
    (square,) = call(
        square_kernel,
        (sign, own, n1, p1, n2, p2),
        [jax.ShapeDtypeStruct((R, 9 * R), bf16)],
        [pltpu.VMEM((R, 5 * R), bf16), pltpu.VMEM((R, 9 * R), f32)],
        5,
        9 * R * R * 2,
    )
    p6 = hop(p4, 2)
    n3 = peer(p4)
    n6 = hop(n4, -2)
    p5 = peer(n4)
    cube, total = call(
        cube_kernel,
        (sign, square, own, n1, p1, n2, p2, n3, p3, n4, p4),
        [jax.ShapeDtypeStruct((R, 13 * R), bf16), jax.ShapeDtypeStruct((R, 13 * R), f32)],
        [pltpu.VMEM((R, 13 * R), f32)],
        18,
        28 * R * R * 2,
    )
    n5 = peer(p6)
    before, last = call(
        far_kernel,
        (sign, cube, total, n5, p5, p6),
        [jax.ShapeDtypeStruct((R, 17 * R), f32), jax.ShapeDtypeStruct((R, R), bf16)],
        [],
        3,
        30 * R * R * 4,
    )
    return edge_call(sign, last, n6, before)


def solution(mesh):
    in_specs = (P("blk", None), P("blk", None))
    out_specs = P("blk", None)
    return jax.shard_map(local, mesh=mesh, in_specs=in_specs, out_specs=out_specs, check_vma=False)
```

```python
import functools
import math

import jax
import jax.numpy as jnp
from jax import lax
from jax.experimental import pallas as pl
from jax.experimental.pallas import tpu as pltpu
from jax.sharding import PartitionSpec as P

B = 512
R = 256
LANES = 128
TILES = 1024 // LANES
ROWS = TILES * R + 16
FIRST_SCALE = 1.0 / math.sqrt(B)
LAST_SCALE = 1.0 / (math.sqrt(B) * math.sqrt(2 * B))
MIB = 1 << 20
CHUNKS = 4


def pack_kernel(adjacency_hbm, weight_hbm, packed_ref, edges, weights, semaphores):
    count = R // CHUNKS
    copies = []
    for chunk in range(CHUNKS):
        rows = slice(chunk * count, (chunk + 1) * count)
        for index, (source, target) in enumerate(((adjacency_hbm, edges), (weight_hbm, weights))):
            copy = pltpu.make_async_copy(source.at[rows, :], target.at[rows, :], semaphores.at[index, chunk])
            copy.start()
            copies.append(copy)
    lane = lax.broadcasted_iota(jnp.int32, (count, LANES), 1)
    diagonals = [jnp.zeros((1, LANES), jnp.float32)] * 2
    for chunk in range(CHUNKS):
        copies[2 * chunk].wait()
        copies[2 * chunk + 1].wait()
        rows = slice(chunk * count, (chunk + 1) * count)
        row = lax.broadcasted_iota(jnp.int32, (count, LANES), 0) + chunk * count

        def tile(index):
            columns = slice(index * LANES, (index + 1) * LANES)
            return edges[rows, columns] == 1, weights[rows, columns].astype(jnp.float32)

        def store(index, value):
            begin = index * R + chunk * count
            packed_ref[begin : begin + count, :] = value.astype(jnp.bfloat16)

        for half in range(2):
            column = lane + half * LANES
            near_edge, near = tile(half)
            far_edge, far = tile(8 + half)
            near = jnp.where(near_edge, near, 0.0)
            far = jnp.where(far_edge, far, 0.0)
            store(half, jnp.where(column >= row, near, far))
            diagonal = jnp.where(column == row, far, 0.0)
            diagonals[half] = diagonals[half] + jnp.sum(diagonal, axis=0, keepdims=True)
        for index in range(2, 8):
            edge, value = tile(index)
            if index in (4, 5):
                edge = edge | (lane + (index - 4) * LANES == row)
            store(index, jnp.where(edge, value, 0.0))
    place = lax.broadcasted_iota(jnp.int32, (16, LANES), 0)
    tail = jnp.where(place == 0, diagonals[0], jnp.where(place == 1, diagonals[1], 0.0))
    packed_ref[TILES * R :, :] = tail.astype(jnp.bfloat16)


def pack(adjacency, weight):
    return pl.pallas_call(
        pack_kernel,
        in_specs=[pl.BlockSpec(memory_space=pltpu.HBM)] * 2,
        out_specs=pl.BlockSpec(memory_space=pltpu.VMEM),
        out_shape=jax.ShapeDtypeStruct((ROWS, LANES), jnp.bfloat16),
        scratch_shapes=[
            pltpu.VMEM((R, 5 * R), jnp.int32),
            pltpu.VMEM((R, 5 * R), jnp.bfloat16),
            pltpu.SemaphoreType.DMA((2, CHUNKS)),
        ],
        compiler_params=pltpu.CompilerParams(vmem_limit_bytes=56 * MIB),
        cost_estimate=pl.CostEstimate(flops=R * 5 * R * 4, bytes_accessed=R * 5 * R * 6 + ROWS * 256, transcendentals=0),
    )(adjacency, weight)


def slot(ref, index):
    begin = index * 2 * R
    return jnp.concatenate([ref[begin : begin + R, :], ref[begin + R : begin + 2 * R, :]], axis=1)


def unpacked(ref):
    row = lax.broadcasted_iota(jnp.int32, (R, R), 0)
    column = lax.broadcasted_iota(jnp.int32, (R, R), 1)
    merged = slot(ref, 0).astype(jnp.float32)
    tail = ref[TILES * R :, :].astype(jnp.float32)
    diagonal = jnp.concatenate([tail[0:1, :], tail[1:2, :]], axis=1)
    first = jnp.where(column >= row, merged, 0.0)
    last = jnp.where(column < row, merged, jnp.where(column == row, diagonal, 0.0))
    return [
        first.astype(jnp.bfloat16),
        slot(ref, 1),
        slot(ref, 2),
        slot(ref, 3),
        last.astype(jnp.bfloat16),
    ]


def block(index):
    return pl.ds(pl.multiple_of(index * R, R), R)


def accumulate(total_ref, left, ref, first_block):
    for offset, right in enumerate(unpacked(ref)):
        where = block(first_block + offset)
        total_ref[:, where] += jnp.dot(left, right, preferred_element_type=jnp.float32)


def near_kernel(sign_ref, own, p1, left_ref, total_ref):
    sign = sign_ref[0]
    for offset, part in enumerate(unpacked(own)):
        left_ref[:, offset * R : (offset + 1) * R] = part
    total_ref[...] = jnp.zeros_like(total_ref)
    for reach, ref in ((0, own), (1, p1)):
        at = reach * sign
        accumulate(total_ref, left_ref[:, block(at + 2)], ref, at + 2)


def add_kernel(reaches, span, sign_ref, left_ref, *refs):
    sign = sign_ref[0]
    before_ref, total_ref = refs[-2:]
    total_ref[...] = before_ref[...]
    for reach, ref in zip(reaches, refs[:-2], strict=True):
        at = reach * sign
        accumulate(total_ref, left_ref[:, block(at + span)], ref, at + span)


def square_kernel(sign_ref, left_ref, d0, n1, p1, n2, p2, before_ref, square_ref, total_ref, work_ref):
    sign = sign_ref[0]
    work_ref[...] = before_ref[...]
    for reach, ref in ((-1, n1), (-2, n2)):
        at = reach * sign
        accumulate(work_ref, left_ref[:, block(at + 2)], ref, at + 2)
    square_ref[...] = (work_ref[...] * FIRST_SCALE).astype(jnp.bfloat16)
    total_ref[...] = jnp.zeros_like(total_ref)
    for reach, ref in ((0, d0), (1, p1), (-1, n1), (2, p2), (-2, n2)):
        at = reach * sign
        accumulate(total_ref, square_ref[:, block(at + 4)], ref, at + 4)


def cube_kernel(sign_ref, left_ref, d0, n1, p1, n2, p2, n3, p3, n4, p4, before_ref, cube_ref, sum_ref, work_ref):
    sign = sign_ref[0]
    work_ref[...] = before_ref[...]
    for reach, ref in ((-3, n3), (-4, n4)):
        at = reach * sign
        accumulate(work_ref, left_ref[:, block(at + 4)], ref, at + 4)
    cube_ref[...] = work_ref[...].astype(jnp.bfloat16)
    sum_ref[...] = jnp.zeros_like(sum_ref)
    known = ((0, d0), (1, p1), (-1, n1), (2, p2), (-2, n2), (3, p3), (-3, n3), (4, p4), (-4, n4))
    for reach, ref in known:
        at = reach * sign
        accumulate(sum_ref, cube_ref[:, block(at + 6)], ref, at + 4)


def far_kernel(sign_ref, cube_ref, sum_ref, p5, p6, out_hbm, partial_ref, last_ref, total_ref, semaphores):
    sign = sign_ref[0]
    half = (1 - sign) // 2
    total_ref[:, : 2 * R] = jnp.zeros((R, 2 * R), jnp.float32)
    total_ref[:, 15 * R :] = jnp.zeros((R, 2 * R), jnp.float32)
    total_ref[:, 2 * R : 15 * R] = sum_ref[...]
    last_ref[:, :R] = cube_ref[:, block(6 - 5 * sign)]
    last_ref[:, R:] = cube_ref[:, block(6 - 6 * sign)]
    for reach, ref in ((5, p5), (6, p6)):
        at = reach * sign
        accumulate(total_ref, cube_ref[:, block(at + 6)], ref, at + 6)
    count = R // CHUNKS
    copies = []
    for chunk in range(CHUNKS):
        rows = slice(chunk * count, (chunk + 1) * count)
        total_ref[rows, :] = total_ref[rows, :] * LAST_SCALE
        columns = pl.ds(pl.multiple_of((1 - half) * 6 * R, R), 11 * R)
        place = (rows, columns)
        copy = pltpu.make_async_copy(total_ref.at[place], out_hbm.at[place], semaphores.at[chunk])
        copy.start()
        copies.append(copy)
    partial_ref[...] = total_ref[:, pl.ds(pl.multiple_of(half * 11 * R, R), 6 * R)]
    for copy in copies:
        copy.wait()


def far_call(sign, cube, total, p5, p6):
    return pl.pallas_call(
        far_kernel,
        in_specs=[pl.BlockSpec(memory_space=pltpu.SMEM)] + [pl.BlockSpec(memory_space=pltpu.VMEM)] * 4,
        out_specs=[pl.BlockSpec(memory_space=pltpu.HBM)] + [pl.BlockSpec(memory_space=pltpu.VMEM)] * 2,
        out_shape=[
            jax.ShapeDtypeStruct((R, 17 * R), jnp.float32),
            jax.ShapeDtypeStruct((R, 6 * R), jnp.float32),
            jax.ShapeDtypeStruct((R, 2 * R), jnp.bfloat16),
        ],
        scratch_shapes=[pltpu.VMEM((R, 17 * R), jnp.float32), pltpu.SemaphoreType.DMA((CHUNKS,))],
        compiler_params=pltpu.CompilerParams(vmem_limit_bytes=20 * MIB),
        cost_estimate=COST,
    )(sign, cube, total, p5, p6)


def edge_kernel(sign_ref, left_ref, n5, n6, partial_ref, before_hbm, out_hbm, result_ref, semaphores):
    del before_hbm
    half = (1 - sign_ref[0]) // 2
    result_ref[...] = partial_ref[...]
    for reach, ref in ((5, n5), (6, n6)):
        left = left_ref[:, (reach - 5) * R : (reach - 4) * R]
        begin = (6 - reach) * (1 - half) + (reach - 5) * half
        for offset, right in enumerate(unpacked(ref)):
            product = jnp.dot(left, right, preferred_element_type=jnp.float32)
            result_ref[:, block(begin + offset)] += product * LAST_SCALE
    copies = []
    for offset in range(3):
        columns = slice(offset * 2 * R, (offset + 1) * 2 * R)
        place = pl.ds(pl.multiple_of((half * 11 + 2 * offset) * R, R), 2 * R)
        copy = pltpu.make_async_copy(result_ref.at[:, columns], out_hbm.at[:, place], semaphores.at[offset])
        copy.start()
        copies.append(copy)
    for copy in copies:
        copy.wait()


def edge_call(sign, left, n5, n6, partial, before):
    vmem = pl.BlockSpec(memory_space=pltpu.VMEM)
    hbm = pl.BlockSpec(memory_space=pltpu.HBM)
    return pl.pallas_call(
        edge_kernel,
        in_specs=[pl.BlockSpec(memory_space=pltpu.SMEM), vmem, vmem, vmem, vmem, hbm],
        out_specs=hbm,
        out_shape=jax.ShapeDtypeStruct(before.shape, jnp.float32),
        scratch_shapes=[pltpu.VMEM((R, 6 * R), jnp.float32), pltpu.SemaphoreType.DMA((3,))],
        input_output_aliases={5: 0},
        compiler_params=pltpu.CompilerParams(vmem_limit_bytes=16 * MIB),
        cost_estimate=COST,
    )(sign, left, n5, n6, partial, before)


COST = pl.CostEstimate(flops=0, bytes_accessed=int(20 * MIB), transcendentals=0)


def call(kernel, arrays, shapes, scratch):
    specs = [pl.BlockSpec(memory_space=pltpu.SMEM)]
    specs += [pl.BlockSpec(memory_space=pltpu.VMEM)] * (len(arrays) - 1)
    return pl.pallas_call(
        kernel,
        in_specs=specs,
        out_specs=[pl.BlockSpec(memory_space=pltpu.VMEM)] * len(shapes),
        out_shape=shapes,
        scratch_shapes=scratch,
        compiler_params=pltpu.CompilerParams(vmem_limit_bytes=24 * MIB),
        cost_estimate=COST,
    )(*arrays)


def local(adjacency, weight):
    size = lax.axis_size("blk")
    parity = lax.rem(lax.axis_index("blk"), 2)
    sign = (1 - 2 * parity).astype(jnp.int32).reshape(1)

    def hop(value, steps):
        pairs = []
        for target in range(size):
            ahead = steps if target % 2 == 0 else -steps
            pairs.append(((target + ahead) % size, target))
        return lax.ppermute(value, "blk", pairs)

    def peer(value):
        return lax.ppermute(value, "blk", [(source, source ^ 1) for source in range(size)])

    tie = lax.optimization_barrier
    f32, bf16 = jnp.float32, jnp.bfloat16
    own = pack(adjacency, weight)
    p2 = hop(own, 2)
    p1 = peer(own)
    held, p1 = tie((own, p1))
    n2 = hop(held, -2)
    left, total = call(
        near_kernel,
        (sign, own, p1),
        [jax.ShapeDtypeStruct((R, 5 * R), bf16), jax.ShapeDtypeStruct((R, 9 * R), f32)],
        [],
    )
    p2, total = tie((p2, total))
    p4 = hop(p2, 2)
    n1 = peer(p2)
    (total,) = call(
        functools.partial(add_kernel, (2,), 2),
        (sign, left, p2, total),
        [jax.ShapeDtypeStruct((R, 9 * R), f32)],
        [],
    )
    n2, total = tie((n2, total))
    n4 = hop(n2, -2)
    p3 = peer(n2)
    square, total = call(
        square_kernel,
        (sign, left, own, n1, p1, n2, p2, total),
        [jax.ShapeDtypeStruct((R, 9 * R), bf16), jax.ShapeDtypeStruct((R, 13 * R), f32)],
        [pltpu.VMEM((R, 9 * R), f32)],
    )
    p4, total = tie((p4, total))
    p6 = hop(p4, 2)
    n3 = peer(p4)
    (total,) = call(
        functools.partial(add_kernel, (3, 4), 4),
        (sign, square, p3, p4, total),
        [jax.ShapeDtypeStruct((R, 13 * R), f32)],
        [],
    )
    n4, total = tie((n4, total))
    n6 = hop(n4, -2)
    p5 = peer(n4)
    cube, total = call(
        cube_kernel,
        (sign, square, own, n1, p1, n2, p2, n3, p3, n4, p4, total),
        [jax.ShapeDtypeStruct((R, 13 * R), bf16), jax.ShapeDtypeStruct((R, 13 * R), f32)],
        [pltpu.VMEM((R, 13 * R), f32)],
    )
    p6, cube = tie((p6, cube))
    n5 = peer(p6)
    before, partial, last = far_call(sign, cube, total, p5, p6)
    n6, last = tie((n6, last))
    return edge_call(sign, last, n5, n6, partial, before)


def solution(mesh):
    in_specs = (P("blk", None), P("blk", None))
    out_specs = P("blk", None)
    return jax.shard_map(local, mesh=mesh, in_specs=in_specs, out_specs=out_specs, check_vma=False)
```

```python
import math

import jax
import jax.numpy as jnp
from jax import lax
from jax.experimental import pallas as pl
from jax.experimental.pallas import tpu as pltpu
from jax.sharding import PartitionSpec as P

B = 512
R = 256
LANES = 128
TILES = 1024 // LANES
ROWS = TILES * R + 16
FIRST_SCALE = 1.0 / math.sqrt(B)
LAST_SCALE = 1.0 / (math.sqrt(B) * math.sqrt(2 * B))
MIB = 1 << 20
CHUNKS = 4


def pack_kernel(adjacency_hbm, weight_hbm, packed_ref, edges, weights, semaphores):
    count = R // CHUNKS
    copies = []
    for chunk in range(CHUNKS):
        rows = slice(chunk * count, (chunk + 1) * count)
        for index, (source, target) in enumerate(((adjacency_hbm, edges), (weight_hbm, weights))):
            copy = pltpu.make_async_copy(source.at[rows, :], target.at[rows, :], semaphores.at[index, chunk])
            copy.start()
            copies.append(copy)
    lane = lax.broadcasted_iota(jnp.int32, (count, LANES), 1)
    diagonals = [jnp.zeros((1, LANES), jnp.float32)] * 2
    for chunk in range(CHUNKS):
        copies[2 * chunk].wait()
        copies[2 * chunk + 1].wait()
        rows = slice(chunk * count, (chunk + 1) * count)
        row = lax.broadcasted_iota(jnp.int32, (count, LANES), 0) + chunk * count

        def tile(index):
            columns = slice(index * LANES, (index + 1) * LANES)
            return edges[rows, columns] == 1, weights[rows, columns].astype(jnp.float32)

        def store(index, value):
            begin = index * R + chunk * count
            packed_ref[begin : begin + count, :] = value.astype(jnp.bfloat16)

        for half in range(2):
            column = lane + half * LANES
            near_edge, near = tile(half)
            far_edge, far = tile(8 + half)
            near = jnp.where(near_edge, near, 0.0)
            far = jnp.where(far_edge, far, 0.0)
            store(half, jnp.where(column >= row, near, far))
            diagonal = jnp.where(column == row, far, 0.0)
            diagonals[half] = diagonals[half] + jnp.sum(diagonal, axis=0, keepdims=True)
        for index in range(2, 8):
            edge, value = tile(index)
            if index in (4, 5):
                edge = edge | (lane + (index - 4) * LANES == row)
            store(index, jnp.where(edge, value, 0.0))
    place = lax.broadcasted_iota(jnp.int32, (16, LANES), 0)
    tail = jnp.where(place == 0, diagonals[0], jnp.where(place == 1, diagonals[1], 0.0))
    packed_ref[TILES * R :, :] = tail.astype(jnp.bfloat16)


def pack(adjacency, weight):
    return pl.pallas_call(
        pack_kernel,
        in_specs=[pl.BlockSpec(memory_space=pltpu.HBM)] * 2,
        out_specs=pl.BlockSpec(memory_space=pltpu.VMEM),
        out_shape=jax.ShapeDtypeStruct((ROWS, LANES), jnp.bfloat16),
        scratch_shapes=[
            pltpu.VMEM((R, 5 * R), jnp.int32),
            pltpu.VMEM((R, 5 * R), jnp.bfloat16),
            pltpu.SemaphoreType.DMA((2, CHUNKS)),
        ],
        compiler_params=pltpu.CompilerParams(vmem_limit_bytes=56 * MIB),
        cost_estimate=pl.CostEstimate(flops=R * 5 * R * 4, bytes_accessed=R * 5 * R * 6 + ROWS * 256, transcendentals=0),
    )(adjacency, weight)


def slot(ref, index):
    begin = index * 2 * R
    return jnp.concatenate([ref[begin : begin + R, :], ref[begin + R : begin + 2 * R, :]], axis=1)


def unpacked(ref):
    row = lax.broadcasted_iota(jnp.int32, (R, R), 0)
    column = lax.broadcasted_iota(jnp.int32, (R, R), 1)
    merged = slot(ref, 0).astype(jnp.float32)
    tail = ref[TILES * R :, :].astype(jnp.float32)
    diagonal = jnp.concatenate([tail[0:1, :], tail[1:2, :]], axis=1)
    first = jnp.where(column >= row, merged, 0.0)
    last = jnp.where(column < row, merged, jnp.where(column == row, diagonal, 0.0))
    return [
        first.astype(jnp.bfloat16),
        slot(ref, 1),
        slot(ref, 2),
        slot(ref, 3),
        last.astype(jnp.bfloat16),
    ]


def block(index):
    return pl.ds(pl.multiple_of(index * R, R), R)


def accumulate(total_ref, left, ref, first_block):
    for offset, right in enumerate(unpacked(ref)):
        where = block(first_block + offset)
        total_ref[:, where] += jnp.dot(left, right, preferred_element_type=jnp.float32)


def near_kernel(sign_ref, own, p0, left_ref, total_ref):
    sign = sign_ref[0]
    for offset, part in enumerate(unpacked(own)):
        left_ref[:, offset * R : (offset + 1) * R] = part
    total_ref[...] = jnp.zeros_like(total_ref)
    for at, ref in ((0, own), (sign, p0)):
        accumulate(total_ref, left_ref[:, block(at + 2)], ref, at + 2)


def square_kernel(sign_ref, left_ref, own, p0, u1, v1, xu1, xv1, before_ref, square_ref, total_ref, work_ref):
    sign = sign_ref[0]
    work_ref[...] = before_ref[...]
    for at, ref in ((-2, u1), (2, v1)):
        accumulate(work_ref, left_ref[:, block(at + 2)], ref, at + 2)

    @pl.when(sign > 0)
    def _():
        accumulate(work_ref, left_ref[:, block(1)], xu1, 1)

    @pl.when(sign < 0)
    def _():
        accumulate(work_ref, left_ref[:, block(3)], xv1, 3)

    square_ref[...] = (work_ref[...] * FIRST_SCALE).astype(jnp.bfloat16)
    total_ref[...] = jnp.zeros_like(total_ref)
    for at, ref in ((0, own), (sign, p0), (-2, u1), (2, v1), (sign - 2, xu1), (sign + 2, xv1)):
        accumulate(total_ref, square_ref[:, block(at + 4)], ref, at + 4)


def cube_kernel(
    sign_ref, left_ref, own, p0, u1, v1, xu1, xv1, u2, v2, xu2, xv2, f3, xf3, before_ref,
    out_hbm, partial_ref, last_ref, work_ref, cube_ref, sum_ref, semaphores,
):
    sign = sign_ref[0]
    half = (1 - sign) // 2
    work_ref[...] = before_ref[...]
    for at, ref in ((-4, u2), (4, v2)):
        accumulate(work_ref, left_ref[:, block(at + 4)], ref, at + 4)

    @pl.when(sign > 0)
    def _():
        accumulate(work_ref, left_ref[:, block(1)], xu2, 1)

    @pl.when(sign < 0)
    def _():
        accumulate(work_ref, left_ref[:, block(7)], xv2, 7)

    cube_ref[...] = (work_ref[...] * LAST_SCALE).astype(jnp.bfloat16)
    last_ref[...] = cube_ref[:, block(6 - 6 * sign)]
    sum_ref[...] = jnp.zeros_like(sum_ref)
    known = ((0, own), (sign, p0), (-2, u1), (2, v1), (sign - 2, xu1), (sign + 2, xv1))
    known += ((-4, u2), (4, v2), (sign - 4, xu2), (sign + 4, xv2), (6 * sign, f3), (-5 * sign, xf3))
    for at, ref in known:
        accumulate(sum_ref, cube_ref[:, block(at + 6)], ref, at + 6)
    count = R // CHUNKS
    copies = []
    for chunk in range(CHUNKS):
        rows = slice(chunk * count, (chunk + 1) * count)
        place = (rows, pl.ds(pl.multiple_of((1 - half) * 5 * R, R), 12 * R))
        copy = pltpu.make_async_copy(sum_ref.at[place], out_hbm.at[place], semaphores.at[chunk])
        copy.start()
        copies.append(copy)
    partial_ref[...] = sum_ref[:, pl.ds(pl.multiple_of(half * 12 * R, R), 5 * R)]
    for copy in copies:
        copy.wait()


def cube_call(*arrays):
    return pl.pallas_call(
        cube_kernel,
        in_specs=[pl.BlockSpec(memory_space=pltpu.SMEM)] + [pl.BlockSpec(memory_space=pltpu.VMEM)] * (len(arrays) - 1),
        out_specs=[pl.BlockSpec(memory_space=pltpu.HBM)] + [pl.BlockSpec(memory_space=pltpu.VMEM)] * 2,
        out_shape=[
            jax.ShapeDtypeStruct((R, 17 * R), jnp.float32),
            jax.ShapeDtypeStruct((R, 5 * R), jnp.float32),
            jax.ShapeDtypeStruct((R, R), jnp.bfloat16),
        ],
        scratch_shapes=[
            pltpu.VMEM((R, 13 * R), jnp.float32),
            pltpu.VMEM((R, 13 * R), jnp.bfloat16),
            pltpu.VMEM((R, 17 * R), jnp.float32),
            pltpu.SemaphoreType.DMA((CHUNKS,)),
        ],
        compiler_params=pltpu.CompilerParams(vmem_limit_bytes=30 * MIB),
        cost_estimate=COST,
    )(*arrays)


def edge_kernel(sign_ref, left_ref, b3, partial_ref, before_hbm, out_hbm, result_ref, semaphores):
    del before_hbm
    half = (1 - sign_ref[0]) // 2
    copies = []
    for offset, right in enumerate(unpacked(b3)):
        columns = slice(offset * R, (offset + 1) * R)
        product = jnp.dot(left_ref[...], right, preferred_element_type=jnp.float32)
        result_ref[:, columns] = partial_ref[:, columns] + product
        copy = pltpu.make_async_copy(
            result_ref.at[:, columns], out_hbm.at[:, block(half * 12 + offset)], semaphores.at[offset]
        )
        copy.start()
        copies.append(copy)
    for copy in copies:
        copy.wait()


def edge_call(sign, left, b3, partial, before):
    vmem = pl.BlockSpec(memory_space=pltpu.VMEM)
    hbm = pl.BlockSpec(memory_space=pltpu.HBM)
    return pl.pallas_call(
        edge_kernel,
        in_specs=[pl.BlockSpec(memory_space=pltpu.SMEM), vmem, vmem, vmem, hbm],
        out_specs=hbm,
        out_shape=jax.ShapeDtypeStruct(before.shape, jnp.float32),
        scratch_shapes=[pltpu.VMEM((R, 5 * R), jnp.float32), pltpu.SemaphoreType.DMA((5,))],
        input_output_aliases={4: 0},
        compiler_params=pltpu.CompilerParams(vmem_limit_bytes=16 * MIB),
        cost_estimate=COST,
    )(sign, left, b3, partial, before)


COST = pl.CostEstimate(flops=0, bytes_accessed=int(0.1 * MIB), transcendentals=0)


def call(kernel, arrays, shapes, scratch):
    specs = [pl.BlockSpec(memory_space=pltpu.SMEM)]
    specs += [pl.BlockSpec(memory_space=pltpu.VMEM)] * (len(arrays) - 1)
    return pl.pallas_call(
        kernel,
        in_specs=specs,
        out_specs=[pl.BlockSpec(memory_space=pltpu.VMEM)] * len(shapes),
        out_shape=shapes,
        scratch_shapes=scratch,
        compiler_params=pltpu.CompilerParams(vmem_limit_bytes=24 * MIB),
        cost_estimate=COST,
    )(*arrays)


def local(adjacency, weight):
    size = lax.axis_size("blk")
    parity = lax.rem(lax.axis_index("blk"), 2)
    sign = (1 - 2 * parity).astype(jnp.int32).reshape(1)

    def hop(value, steps):
        pairs = []
        for target in range(size):
            ahead = steps if target % 2 == 0 else -steps
            pairs.append(((target + ahead) % size, target))
        return lax.ppermute(value, "blk", pairs)

    def shifted(value, steps):
        return lax.ppermute(value, "blk", [((target + steps) % size, target) for target in range(size)])

    def peer(value):
        return lax.ppermute(value, "blk", [(source, source ^ 1) for source in range(size)])

    tie = lax.optimization_barrier
    f32, bf16 = jnp.float32, jnp.bfloat16
    own = pack(adjacency, weight)
    u1 = shifted(own, -2)
    v1 = shifted(own, 2)
    p0 = peer(own)
    left, total = call(
        near_kernel,
        (sign, own, p0),
        [jax.ShapeDtypeStruct((R, 5 * R), bf16), jax.ShapeDtypeStruct((R, 9 * R), f32)],
        [],
    )
    held, total = tie((own, total))
    f3 = hop(held, 6)
    u2 = shifted(u1, -2)
    v2 = shifted(v1, 2)
    xu1 = peer(u1)
    xv1 = peer(v1)
    f3, total = tie((f3, total))
    square, total = call(
        square_kernel,
        (sign, left, own, p0, u1, v1, xu1, xv1, total),
        [jax.ShapeDtypeStruct((R, 9 * R), bf16), jax.ShapeDtypeStruct((R, 13 * R), f32)],
        [pltpu.VMEM((R, 9 * R), f32)],
    )
    held, u2, v2, total = tie((held, u2, v2, total))
    b3 = hop(held, -6)
    xu2 = peer(u2)
    xv2 = peer(v2)
    xf3 = peer(f3)
    before, partial, last = cube_call(
        sign, square, own, p0, u1, v1, xu1, xv1, u2, v2, xu2, xv2, f3, xf3, total
    )
    return edge_call(sign, last, b3, partial, before)


def solution(mesh):
    in_specs = (P("blk", None), P("blk", None))
    out_specs = P("blk", None)
    return jax.shard_map(local, mesh=mesh, in_specs=in_specs, out_specs=out_specs, check_vma=False)
```

```python
import math

import jax
import jax.numpy as jnp
from jax import lax
from jax.experimental import pallas as pl
from jax.experimental.pallas import tpu as pltpu
from jax.sharding import PartitionSpec as P

B = 512
R = 256
LANES = 128
TILES = 1024 // LANES
ROWS = TILES * R + 16
FIRST_SCALE = 1.0 / math.sqrt(B)
LAST_SCALE = 1.0 / (math.sqrt(B) * math.sqrt(2 * B))
MIB = 1 << 20


def pack_kernel(adjacency_hbm, weight_hbm, packed_hbm, edges, weights, packed, in_semaphores, out_semaphores):
    copies = {}
    for part in (0, 4, 1, 2, 3):
        columns = slice(part * R, (part + 1) * R)
        for index, (source, target) in enumerate(((adjacency_hbm, edges), (weight_hbm, weights))):
            semaphore = in_semaphores.at[index, part]
            copies[index, part] = pltpu.make_async_copy(source.at[:, columns], target.at[:, columns], semaphore)
            copies[index, part].start()
    row = lax.broadcasted_iota(jnp.int32, (R, LANES), 0)
    lane = lax.broadcasted_iota(jnp.int32, (R, LANES), 1)
    leaving = []

    def leave(rows, index):
        copy = pltpu.make_async_copy(packed.at[rows, :], packed_hbm.at[rows, :], out_semaphores.at[index])
        copy.start()
        leaving.append(copy)

    def arrive(part):
        copies[0, part].wait()
        copies[1, part].wait()

    def tile(index):
        columns = slice(index * LANES, (index + 1) * LANES)
        return edges[:, columns] == 1, weights[:, columns].astype(jnp.float32)

    arrive(0)
    arrive(4)
    place = lax.broadcasted_iota(jnp.int32, (16, LANES), 0)
    tail = jnp.zeros((16, LANES), jnp.float32)
    for half in range(2):
        column = lane + half * LANES
        near_edge, near = tile(half)
        far_edge, far = tile(8 + half)
        near = jnp.where(near_edge, near, 0.0)
        far = jnp.where(far_edge, far, 0.0)
        packed[half * R : (half + 1) * R, :] = jnp.where(column >= row, near, far).astype(jnp.bfloat16)
        diagonal = jnp.sum(jnp.where(column == row, far, 0.0), axis=0, keepdims=True)
        tail = jnp.where(place == half, diagonal, tail)
    packed[TILES * R :, :] = tail.astype(jnp.bfloat16)
    leave(slice(0, 2 * R), 0)
    leave(slice(TILES * R, ROWS), 4)
    for part in (1, 2, 3):
        arrive(part)
        for half in range(2):
            index = 2 * part + half
            edge, value = tile(index)
            if part == 2:
                edge = edge | (lane + half * LANES == row)
            packed[index * R : (index + 1) * R, :] = jnp.where(edge, value, 0.0).astype(jnp.bfloat16)
        leave(slice(2 * part * R, 2 * (part + 1) * R), part)
    for copy in leaving:
        copy.wait()


def pack(adjacency, weight):
    hbm = pl.BlockSpec(memory_space=pltpu.HBM)
    return pl.pallas_call(
        pack_kernel,
        in_specs=[hbm, hbm],
        out_specs=hbm,
        out_shape=jax.ShapeDtypeStruct((ROWS, LANES), jnp.bfloat16),
        scratch_shapes=[
            pltpu.VMEM((R, 5 * R), jnp.int32),
            pltpu.VMEM((R, 5 * R), jnp.bfloat16),
            pltpu.VMEM((ROWS, LANES), jnp.bfloat16),
            pltpu.SemaphoreType.DMA((2, 5)),
            pltpu.SemaphoreType.DMA((5,)),
        ],
        compiler_params=pltpu.CompilerParams(vmem_limit_bytes=56 * MIB),
        cost_estimate=pl.CostEstimate(flops=R * 5 * R * 4, bytes_accessed=R * 5 * R * 6 + ROWS * 256, transcendentals=0),
    )(adjacency, weight)


def slot(ref, index):
    begin = index * 2 * R
    return jnp.concatenate([ref[begin : begin + R, :], ref[begin + R : begin + 2 * R, :]], axis=1)


def unpacked(ref):
    row = lax.broadcasted_iota(jnp.int32, (R, R), 0)
    column = lax.broadcasted_iota(jnp.int32, (R, R), 1)
    merged = slot(ref, 0).astype(jnp.float32)
    tail = ref[TILES * R :, :].astype(jnp.float32)
    diagonal = jnp.concatenate([tail[0:1, :], tail[1:2, :]], axis=1)
    first = jnp.where(column >= row, merged, 0.0)
    last = jnp.where(column < row, merged, jnp.where(column == row, diagonal, 0.0))
    return [
        first.astype(jnp.bfloat16),
        slot(ref, 1),
        slot(ref, 2),
        slot(ref, 3),
        last.astype(jnp.bfloat16),
    ]


def block(index):
    return pl.ds(pl.multiple_of(index * R, R), R)


def accumulate(total_ref, left, ref, first_block):
    for offset, right in enumerate(unpacked(ref)):
        where = block(first_block + offset)
        total_ref[:, where] += jnp.dot(left, right, preferred_element_type=jnp.float32)


def near_kernel(sign_ref, own, p0, left_ref, total_ref):
    sign = sign_ref[0]
    for offset, part in enumerate(unpacked(own)):
        left_ref[:, offset * R : (offset + 1) * R] = part
    total_ref[...] = jnp.zeros_like(total_ref)
    for at, ref in ((0, own), (sign, p0)):
        accumulate(total_ref, left_ref[:, block(at + 2)], ref, at + 2)


def square_kernel(sign_ref, left_ref, own, p0, v1, u1, xv1, xu1, before_ref, square_ref, total_ref, work_ref):
    sign = sign_ref[0]
    work_ref[...] = before_ref[...]
    for at, ref in ((-2, u1), (2, v1)):
        accumulate(work_ref, left_ref[:, block(at + 2)], ref, at + 2)

    @pl.when(sign > 0)
    def _():
        accumulate(work_ref, left_ref[:, block(1)], xu1, 1)

    @pl.when(sign < 0)
    def _():
        accumulate(work_ref, left_ref[:, block(3)], xv1, 3)

    square_ref[...] = (work_ref[...] * FIRST_SCALE).astype(jnp.bfloat16)
    total_ref[...] = jnp.zeros_like(total_ref)
    for at, ref in ((0, own), (sign, p0), (-2, u1), (2, v1), (sign - 2, xu1), (sign + 2, xv1)):
        accumulate(total_ref, square_ref[:, block(at + 4)], ref, at + 4)


def piece(ref, index):
    if index in (1, 2, 3):
        return slot(ref, index)
    row = lax.broadcasted_iota(jnp.int32, (R, R), 0)
    column = lax.broadcasted_iota(jnp.int32, (R, R), 1)
    merged = slot(ref, 0).astype(jnp.float32)
    if index == 0:
        return jnp.where(column >= row, merged, 0.0).astype(jnp.bfloat16)
    tail = ref[TILES * R :, :].astype(jnp.float32)
    diagonal = jnp.concatenate([tail[0:1, :], tail[1:2, :]], axis=1)
    return jnp.where(column < row, merged, jnp.where(column == row, diagonal, 0.0)).astype(jnp.bfloat16)


def band_dot(lefts, rows, at):
    places = [place for place in sorted(rows) if abs(at - place) <= 2]
    left = jnp.concatenate([lefts[place][...] for place in places], axis=1)
    right = jnp.concatenate([piece(rows[place], at - place + 2) for place in places], axis=0)
    return jnp.dot(left, right, preferred_element_type=jnp.float32)


def columns_of(ref, place, span):
    return ref.at[:, (place + span) * R : (place + span + 1) * R]


def both_cores(sign_ref, body):
    for sign in (1, -1):
        pl.when(sign_ref[0] == sign)(lambda sign=sign: body(sign))


def forward_kernel(sign_ref, left_ref, own, p0, v1, u1, xv1, xu1, v2, u2, f3, before_ref, cube_ref, rest_ref, sum_ref):
    def body(sign):
        rows = {0: own, sign: p0, -2: u1, 2: v1, sign - 2: xu1, sign + 2: xv1, -4: u2, 4: v2, 6 * sign: f3}
        outer = {place: rows[place] for place in (-4, 4)}
        for at in range(-6, 7):
            value = columns_of(before_ref, at, 6)[...]
            if abs(at) >= 2:
                value = value + band_dot({p: columns_of(left_ref, p, 4) for p in outer}, outer, at)
            if -6 < at * sign < 0:
                columns_of(rest_ref, at * sign, 5)[...] = value
            else:
                columns_of(cube_ref, at, 6)[...] = (value * LAST_SCALE).astype(jnp.bfloat16)
        ready = {place * sign: rows[place * sign] for place in (0, 1, 2, 3, 4, 6)}
        for at in range(-2, 9):
            lefts = {place: columns_of(cube_ref, place, 6) for place in ready}
            columns_of(sum_ref, at * sign, 8)[...] = band_dot(lefts, ready, at * sign)

    both_cores(sign_ref, body)


def edge_kernel(sign_ref, cube_ref, b3, product_ref):
    left = cube_ref[:, block(6 - 6 * sign_ref[0])]
    for index in range(5):
        right = piece(b3, index)
        product_ref[:, index * R : (index + 1) * R] = jnp.dot(left, right, preferred_element_type=jnp.float32)


def last_kernel(
    sign_ref, left_ref, v1, u1, xv1, xu1, v2, u2, xv2, xu2, xf3, edge_ref, cube_ref, rest_ref, sum_ref,
    out_hbm, late_ref, result_ref, semaphores,
):
    def body(sign):
        rows = {-2: u1, 2: v1, sign - 2: xu1, sign + 2: xv1, -4: u2, 4: v2, sign - 4: xu2, sign + 4: xv2}
        rows[-5 * sign] = xf3
        copies = []

        def leave(at, ref):
            place = columns_of(out_hbm, at, 8)
            copy = pltpu.make_async_copy(columns_of(ref, at, 8), place, semaphores.at[at + 8])
            copy.start()
            copies.append(copy)

        for at in (2, 8):
            leave(at * sign, sum_ref)
        third = {-3 * sign: rows[-3 * sign]}
        lefts = {5 * sign: columns_of(cube_ref, 5 * sign, 6)}
        for at in range(-5, 0):
            value = columns_of(rest_ref, at, 5)[...]
            value = value + band_dot({-3 * sign: columns_of(left_ref, -3 * sign, 4)}, third, at * sign)
            columns_of(late_ref, at, 5)[...] = (value * LAST_SCALE).astype(jnp.bfloat16)
            lefts[at * sign] = columns_of(late_ref, at, 5)
        ready = {place: rows[place] for place in lefts}
        for at in (3, 4, 5, 6, 7, 1, 0, -1, -2, -3, -4, -5, -6, -7, -8):
            if at > -8:
                value = band_dot(lefts, ready, at * sign)
            else:
                value = jnp.zeros((R, R), jnp.float32)
            if at <= -4:
                value = value + columns_of(edge_ref, at * sign + 6 * sign, 2)[...]
            if at >= -2:
                value = value + columns_of(sum_ref, at * sign, 8)[...]
            columns_of(result_ref, at * sign, 8)[...] = value
            leave(at * sign, result_ref)
        for copy in copies:
            copy.wait()

    both_cores(sign_ref, body)


def last_call(*arrays):
    return pl.pallas_call(
        last_kernel,
        in_specs=[pl.BlockSpec(memory_space=pltpu.SMEM)] + [pl.BlockSpec(memory_space=pltpu.VMEM)] * (len(arrays) - 1),
        out_specs=pl.BlockSpec(memory_space=pltpu.HBM),
        out_shape=jax.ShapeDtypeStruct((R, 17 * R), jnp.float32),
        scratch_shapes=[
            pltpu.VMEM((R, 5 * R), jnp.bfloat16),
            pltpu.VMEM((R, 17 * R), jnp.float32),
            pltpu.SemaphoreType.DMA((17,)),
        ],
        compiler_params=pltpu.CompilerParams(vmem_limit_bytes=30 * MIB),
        cost_estimate=COST,
    )(*arrays)


COST = pl.CostEstimate(flops=0, bytes_accessed=int(0.1 * MIB), transcendentals=0)


def call(kernel, arrays, shapes, scratch):
    specs = [pl.BlockSpec(memory_space=pltpu.SMEM)]
    specs += [pl.BlockSpec(memory_space=pltpu.VMEM)] * (len(arrays) - 1)
    return pl.pallas_call(
        kernel,
        in_specs=specs,
        out_specs=[pl.BlockSpec(memory_space=pltpu.VMEM)] * len(shapes),
        out_shape=shapes,
        scratch_shapes=scratch,
        compiler_params=pltpu.CompilerParams(vmem_limit_bytes=24 * MIB),
        cost_estimate=COST,
    )(*arrays)


def local(adjacency, weight):
    size = lax.axis_size("blk")
    parity = lax.rem(lax.axis_index("blk"), 2)
    sign = (1 - 2 * parity).astype(jnp.int32).reshape(1)

    def hop(value, steps):
        pairs = []
        for target in range(size):
            ahead = steps if target % 2 == 0 else -steps
            pairs.append(((target + ahead) % size, target))
        return lax.ppermute(value, "blk", pairs)

    def shifted(value, steps):
        return lax.ppermute(value, "blk", [((target + steps) % size, target) for target in range(size)])

    def peer(value):
        return lax.ppermute(value, "blk", [(source, source ^ 1) for source in range(size)])

    tie = lax.optimization_barrier
    f32, bf16 = jnp.float32, jnp.bfloat16
    own = pack(adjacency, weight)
    u1 = shifted(own, -2)
    v1 = shifted(own, 2)
    p0 = peer(own)
    left, total = call(
        near_kernel,
        (sign, own, p0),
        [jax.ShapeDtypeStruct((R, 5 * R), bf16), jax.ShapeDtypeStruct((R, 9 * R), f32)],
        [],
    )
    held, total = tie((own, total))
    f3 = hop(held, 6)
    u2 = shifted(u1, -2)
    v2 = shifted(v1, 2)
    xu1 = peer(u1)
    xv1 = peer(v1)
    f3, total = tie((f3, total))
    square, total = call(
        square_kernel,
        (sign, left, own, p0, v1, u1, xv1, xu1, total),
        [jax.ShapeDtypeStruct((R, 9 * R), bf16), jax.ShapeDtypeStruct((R, 13 * R), f32)],
        [pltpu.VMEM((R, 9 * R), f32)],
    )
    held, total = tie((held, total))
    b3 = hop(held, -6)
    u2, v2, total = tie((u2, v2, total))
    xu2 = peer(u2)
    xv2 = peer(v2)
    xf3 = peer(f3)
    cube, rest, total = call(
        forward_kernel,
        (sign, square, own, p0, v1, u1, xv1, xu1, v2, u2, f3, total),
        [
            jax.ShapeDtypeStruct((R, 13 * R), bf16),
            jax.ShapeDtypeStruct((R, 5 * R), f32),
            jax.ShapeDtypeStruct((R, 17 * R), f32),
        ],
        [],
    )
    (edge,) = call(edge_kernel, (sign, cube, b3), [jax.ShapeDtypeStruct((R, 5 * R), f32)], [])
    return last_call(sign, square, v1, u1, xv1, xu1, v2, u2, xv2, xu2, xf3, edge, cube, rest, total)


def solution(mesh):
    in_specs = (P("blk", None), P("blk", None))
    out_specs = P("blk", None)
    return jax.shard_map(local, mesh=mesh, in_specs=in_specs, out_specs=out_specs, check_vma=False)
```

```python
import math

import jax
import jax.numpy as jnp
from jax import lax
from jax.experimental import pallas as pl
from jax.experimental.pallas import tpu as pltpu
from jax.sharding import PartitionSpec as P

B = 512
R = 256
LANES = 128
TILES = 1024 // LANES
ROWS = TILES * R + 16
FIRST_SCALE = 1.0 / math.sqrt(B)
LAST_SCALE = 1.0 / (math.sqrt(B) * math.sqrt(2 * B))
MIB = 1 << 20


def pack_kernel(adjacency_hbm, weight_hbm, packed_hbm, edges, weights, packed, in_semaphores, out_semaphores):
    copies = {}
    for part in (0, 4, 1, 2, 3):
        columns = slice(part * R, (part + 1) * R)
        for index, (source, target) in enumerate(((adjacency_hbm, edges), (weight_hbm, weights))):
            semaphore = in_semaphores.at[index, part]
            copies[index, part] = pltpu.make_async_copy(source.at[:, columns], target.at[:, columns], semaphore)
            copies[index, part].start()
    row = lax.broadcasted_iota(jnp.int32, (R, LANES), 0)
    lane = lax.broadcasted_iota(jnp.int32, (R, LANES), 1)
    leaving = []

    def leave(rows, index):
        copy = pltpu.make_async_copy(packed.at[rows, :], packed_hbm.at[rows, :], out_semaphores.at[index])
        copy.start()
        leaving.append(copy)

    def arrive(part):
        copies[0, part].wait()
        copies[1, part].wait()

    def tile(index):
        columns = slice(index * LANES, (index + 1) * LANES)
        return edges[:, columns] == 1, weights[:, columns].astype(jnp.float32)

    arrive(0)
    arrive(4)
    place = lax.broadcasted_iota(jnp.int32, (16, LANES), 0)
    tail = jnp.zeros((16, LANES), jnp.float32)
    for half in range(2):
        column = lane + half * LANES
        near_edge, near = tile(half)
        far_edge, far = tile(8 + half)
        near = jnp.where(near_edge, near, 0.0)
        far = jnp.where(far_edge, far, 0.0)
        packed[half * R : (half + 1) * R, :] = jnp.where(column >= row, near, far).astype(jnp.bfloat16)
        diagonal = jnp.sum(jnp.where(column == row, far, 0.0), axis=0, keepdims=True)
        tail = jnp.where(place == half, diagonal, tail)
    packed[TILES * R :, :] = tail.astype(jnp.bfloat16)
    leave(slice(0, 2 * R), 0)
    leave(slice(TILES * R, ROWS), 4)
    for part in (1, 2, 3):
        arrive(part)
        for half in range(2):
            index = 2 * part + half
            edge, value = tile(index)
            if part == 2:
                edge = edge | (lane + half * LANES == row)
            packed[index * R : (index + 1) * R, :] = jnp.where(edge, value, 0.0).astype(jnp.bfloat16)
        leave(slice(2 * part * R, 2 * (part + 1) * R), part)
    for copy in leaving:
        copy.wait()


def pack(adjacency, weight):
    hbm = pl.BlockSpec(memory_space=pltpu.HBM)
    return pl.pallas_call(
        pack_kernel,
        in_specs=[hbm, hbm],
        out_specs=hbm,
        out_shape=jax.ShapeDtypeStruct((ROWS, LANES), jnp.bfloat16),
        scratch_shapes=[
            pltpu.VMEM((R, 5 * R), jnp.int32),
            pltpu.VMEM((R, 5 * R), jnp.bfloat16),
            pltpu.VMEM((ROWS, LANES), jnp.bfloat16),
            pltpu.SemaphoreType.DMA((2, 5)),
            pltpu.SemaphoreType.DMA((5,)),
        ],
        compiler_params=pltpu.CompilerParams(vmem_limit_bytes=53 * MIB),
        cost_estimate=pl.CostEstimate(flops=R * 5 * R * 4, bytes_accessed=R * 5 * R * 6 + ROWS * 256, transcendentals=0),
    )(adjacency, weight)


def slot(ref, index):
    begin = index * 2 * R
    return jnp.concatenate([ref[begin : begin + R, :], ref[begin + R : begin + 2 * R, :]], axis=1)


def unpacked(ref):
    row = lax.broadcasted_iota(jnp.int32, (R, R), 0)
    column = lax.broadcasted_iota(jnp.int32, (R, R), 1)
    merged = slot(ref, 0).astype(jnp.float32)
    tail = ref[TILES * R :, :].astype(jnp.float32)
    diagonal = jnp.concatenate([tail[0:1, :], tail[1:2, :]], axis=1)
    first = jnp.where(column >= row, merged, 0.0)
    last = jnp.where(column < row, merged, jnp.where(column == row, diagonal, 0.0))
    return [
        first.astype(jnp.bfloat16),
        slot(ref, 1),
        slot(ref, 2),
        slot(ref, 3),
        last.astype(jnp.bfloat16),
    ]


def block(index):
    return pl.ds(pl.multiple_of(index * R, R), R)


def accumulate(total_ref, left, ref, first_block):
    for offset, right in enumerate(unpacked(ref)):
        where = block(first_block + offset)
        total_ref[:, where] += jnp.dot(left, right, preferred_element_type=jnp.float32)


def near_kernel(sign_ref, own, p0, left_ref, total_ref):
    sign = sign_ref[0]
    for offset, part in enumerate(unpacked(own)):
        left_ref[:, offset * R : (offset + 1) * R] = part
    total_ref[...] = jnp.zeros_like(total_ref)
    for at, ref in ((0, own), (sign, p0)):
        accumulate(total_ref, left_ref[:, block(at + 2)], ref, at + 2)


def square_kernel(sign_ref, left_ref, own, p0, v1, u1, xv1, xu1, before_ref, square_ref, total_ref, work_ref):
    sign = sign_ref[0]
    work_ref[...] = before_ref[...]
    for at, ref in ((-2, u1), (2, v1)):
        accumulate(work_ref, left_ref[:, block(at + 2)], ref, at + 2)

    @pl.when(sign > 0)
    def _():
        accumulate(work_ref, left_ref[:, block(1)], xu1, 1)

    @pl.when(sign < 0)
    def _():
        accumulate(work_ref, left_ref[:, block(3)], xv1, 3)

    square_ref[...] = (work_ref[...] * FIRST_SCALE).astype(jnp.bfloat16)
    total_ref[...] = jnp.zeros_like(total_ref)
    for at, ref in ((0, own), (sign, p0), (-2, u1), (2, v1), (sign - 2, xu1), (sign + 2, xv1)):
        accumulate(total_ref, square_ref[:, block(at + 4)], ref, at + 4)


def piece(ref, index):
    if index in (1, 2, 3):
        return slot(ref, index)
    row = lax.broadcasted_iota(jnp.int32, (R, R), 0)
    column = lax.broadcasted_iota(jnp.int32, (R, R), 1)
    merged = slot(ref, 0).astype(jnp.float32)
    if index == 0:
        return jnp.where(column >= row, merged, 0.0).astype(jnp.bfloat16)
    tail = ref[TILES * R :, :].astype(jnp.float32)
    diagonal = jnp.concatenate([tail[0:1, :], tail[1:2, :]], axis=1)
    return jnp.where(column < row, merged, jnp.where(column == row, diagonal, 0.0)).astype(jnp.bfloat16)


def band_dot(lefts, rows, at):
    places = [place for place in sorted(rows) if abs(at - place) <= 2]
    left = jnp.concatenate([lefts[place][...] for place in places], axis=1)
    right = jnp.concatenate([piece(rows[place], at - place + 2) for place in places], axis=0)
    return jnp.dot(left, right, preferred_element_type=jnp.float32)


def columns_of(ref, place, span):
    return ref.at[:, (place + span) * R : (place + span + 1) * R]


def both_cores(sign_ref, body):
    for sign in (1, -1):
        pl.when(sign_ref[0] == sign)(lambda sign=sign: body(sign))


def forward_kernel(sign_ref, left_ref, own, p0, v1, u1, xv1, xu1, v2, u2, f3, before_ref, cube_ref, rest_ref, sum_ref):
    def body(sign):
        rows = {0: own, sign: p0, -2: u1, 2: v1, sign - 2: xu1, sign + 2: xv1, -4: u2, 4: v2, 6 * sign: f3}
        outer = {place: rows[place] for place in (-4, 4)}
        for at in range(-6, 7):
            value = columns_of(before_ref, at, 6)[...]
            if abs(at) >= 2:
                value = value + band_dot({p: columns_of(left_ref, p, 4) for p in outer}, outer, at)
            if -6 < at * sign < 0:
                columns_of(rest_ref, at * sign, 5)[...] = value
            else:
                columns_of(cube_ref, at, 6)[...] = (value * LAST_SCALE).astype(jnp.bfloat16)
        ready = {place * sign: rows[place * sign] for place in (0, 1, 2, 3, 4, 6)}
        for at in range(-2, 9):
            lefts = {place: columns_of(cube_ref, place, 6) for place in ready}
            columns_of(sum_ref, at * sign, 8)[...] = band_dot(lefts, ready, at * sign)

    both_cores(sign_ref, body)


def edge_kernel(sign_ref, cube_ref, b3, product_ref):
    left = cube_ref[:, block(6 - 6 * sign_ref[0])]
    for index in range(5):
        right = piece(b3, index)
        product_ref[:, index * R : (index + 1) * R] = jnp.dot(left, right, preferred_element_type=jnp.float32)


def last_kernel(
    sign_ref, left_ref, v1, u1, xv1, xu1, v2, u2, xv2, xu2, xf3, edge_ref, cube_ref, rest_ref, sum_ref,
    out_hbm, late_ref, result_ref, semaphores,
):
    def body(sign):
        rows = {-2: u1, 2: v1, sign - 2: xu1, sign + 2: xv1, -4: u2, 4: v2, sign - 4: xu2, sign + 4: xv2}
        rows[-5 * sign] = xf3
        copies = []

        def leave(at, ref):
            place = columns_of(out_hbm, at, 8)
            copy = pltpu.make_async_copy(columns_of(ref, at, 8), place, semaphores.at[at + 8])
            copy.start()
            copies.append(copy)

        for at in (2, 8):
            leave(at * sign, sum_ref)
        third = {-3 * sign: rows[-3 * sign]}
        lefts = {5 * sign: columns_of(cube_ref, 5 * sign, 6)}

        def finish(at):
            value = jnp.zeros((R, R), jnp.float32)
            if at > -8:
                value = band_dot(lefts, {place: rows[place] for place in lefts}, at * sign)
            if at <= -4:
                value = value + columns_of(edge_ref, at * sign + 6 * sign, 2)[...]
            if at >= -2:
                value = value + columns_of(sum_ref, at * sign, 8)[...]
            columns_of(result_ref, at * sign, 8)[...] = value
            leave(at * sign, result_ref)

        for at in (3, 4, 5, 6, 7):
            finish(at)
        for at in range(-5, 0):
            value = columns_of(rest_ref, at, 5)[...]
            value = value + band_dot({-3 * sign: columns_of(left_ref, -3 * sign, 4)}, third, at * sign)
            columns_of(late_ref, at, 5)[...] = (value * LAST_SCALE).astype(jnp.bfloat16)
            lefts[at * sign] = columns_of(late_ref, at, 5)
        for at in (1, 0, -1, -2, -3, -4, -5, -6, -7, -8):
            finish(at)
        for copy in copies:
            copy.wait()

    both_cores(sign_ref, body)


def last_call(*arrays):
    return pl.pallas_call(
        last_kernel,
        in_specs=[pl.BlockSpec(memory_space=pltpu.SMEM)] + [pl.BlockSpec(memory_space=pltpu.VMEM)] * (len(arrays) - 1),
        out_specs=pl.BlockSpec(memory_space=pltpu.HBM),
        out_shape=jax.ShapeDtypeStruct((R, 17 * R), jnp.float32),
        scratch_shapes=[
            pltpu.VMEM((R, 5 * R), jnp.bfloat16),
            pltpu.VMEM((R, 17 * R), jnp.float32),
            pltpu.SemaphoreType.DMA((17,)),
        ],
        compiler_params=pltpu.CompilerParams(vmem_limit_bytes=30 * MIB),
        cost_estimate=COST,
    )(*arrays)


COST = pl.CostEstimate(flops=0, bytes_accessed=int(0.1 * MIB), transcendentals=0)


def call(kernel, arrays, shapes, scratch):
    specs = [pl.BlockSpec(memory_space=pltpu.SMEM)]
    specs += [pl.BlockSpec(memory_space=pltpu.VMEM)] * (len(arrays) - 1)
    return pl.pallas_call(
        kernel,
        in_specs=specs,
        out_specs=[pl.BlockSpec(memory_space=pltpu.VMEM)] * len(shapes),
        out_shape=shapes,
        scratch_shapes=scratch,
        compiler_params=pltpu.CompilerParams(vmem_limit_bytes=24 * MIB),
        cost_estimate=COST,
    )(*arrays)


def local(adjacency, weight):
    size = lax.axis_size("blk")
    parity = lax.rem(lax.axis_index("blk"), 2)
    sign = (1 - 2 * parity).astype(jnp.int32).reshape(1)

    def hop(value, steps):
        pairs = []
        for target in range(size):
            ahead = steps if target % 2 == 0 else -steps
            pairs.append(((target + ahead) % size, target))
        return lax.ppermute(value, "blk", pairs)

    def shifted(value, steps):
        return lax.ppermute(value, "blk", [((target + steps) % size, target) for target in range(size)])

    def peer(value):
        return lax.ppermute(value, "blk", [(source, source ^ 1) for source in range(size)])

    tie = lax.optimization_barrier
    f32, bf16 = jnp.float32, jnp.bfloat16
    own = pack(adjacency, weight)
    u1 = shifted(own, -2)
    v1 = shifted(own, 2)
    p0 = peer(own)
    left, total = call(
        near_kernel,
        (sign, own, p0),
        [jax.ShapeDtypeStruct((R, 5 * R), bf16), jax.ShapeDtypeStruct((R, 9 * R), f32)],
        [],
    )
    held, total = tie((own, total))
    f3 = hop(held, 6)
    u2 = shifted(u1, -2)
    v2 = shifted(v1, 2)
    xu1 = peer(u1)
    xv1 = peer(v1)
    f3, total = tie((f3, total))
    square, total = call(
        square_kernel,
        (sign, left, own, p0, v1, u1, xv1, xu1, total),
        [jax.ShapeDtypeStruct((R, 9 * R), bf16), jax.ShapeDtypeStruct((R, 13 * R), f32)],
        [pltpu.VMEM((R, 9 * R), f32)],
    )
    held, total = tie((held, total))
    b3 = hop(held, -6)
    u2, v2, total = tie((u2, v2, total))
    xu2 = peer(u2)
    xv2 = peer(v2)
    xf3 = peer(f3)
    cube, rest, total = call(
        forward_kernel,
        (sign, square, own, p0, v1, u1, xv1, xu1, v2, u2, f3, total),
        [
            jax.ShapeDtypeStruct((R, 13 * R), bf16),
            jax.ShapeDtypeStruct((R, 5 * R), f32),
            jax.ShapeDtypeStruct((R, 17 * R), f32),
        ],
        [],
    )
    (edge,) = call(edge_kernel, (sign, cube, b3), [jax.ShapeDtypeStruct((R, 5 * R), f32)], [])
    return last_call(sign, square, v1, u1, xv1, xu1, v2, u2, xv2, xu2, xf3, edge, cube, rest, total)


def solution(mesh):
    in_specs = (P("blk", None), P("blk", None))
    out_specs = P("blk", None)
    return jax.shard_map(local, mesh=mesh, in_specs=in_specs, out_specs=out_specs, check_vma=False)
```

```python
import math

import jax
import jax.numpy as jnp
from jax import lax
from jax.experimental import pallas as pl
from jax.experimental.pallas import tpu as pltpu
from jax.sharding import PartitionSpec as P

B = 512
R = 256
LANES = 128
TILES = 1024 // LANES
ROWS = TILES * R + 16
FIRST_SCALE = 1.0 / math.sqrt(B)
LAST_SCALE = 1.0 / (math.sqrt(B) * math.sqrt(2 * B))
MIB = 1 << 20


def pack_kernel(adjacency_hbm, weight_hbm, packed_hbm, edges, weights, packed, in_semaphores, out_semaphores):
    copies = {}
    for part in (0, 4, 1, 2, 3):
        columns = slice(part * R, (part + 1) * R)
        for index, (source, target) in enumerate(((adjacency_hbm, edges), (weight_hbm, weights))):
            semaphore = in_semaphores.at[index, part]
            copies[index, part] = pltpu.make_async_copy(source.at[:, columns], target.at[:, columns], semaphore)
            copies[index, part].start()
    row = lax.broadcasted_iota(jnp.int32, (R, LANES), 0)
    lane = lax.broadcasted_iota(jnp.int32, (R, LANES), 1)
    leaving = []

    def leave(rows, index):
        copy = pltpu.make_async_copy(packed.at[rows, :], packed_hbm.at[rows, :], out_semaphores.at[index])
        copy.start()
        leaving.append(copy)

    def arrive(part):
        copies[0, part].wait()
        copies[1, part].wait()

    def tile(index):
        columns = slice(index * LANES, (index + 1) * LANES)
        return edges[:, columns] == 1, weights[:, columns].astype(jnp.float32)

    arrive(0)
    arrive(4)
    place = lax.broadcasted_iota(jnp.int32, (16, LANES), 0)
    tail = jnp.zeros((16, LANES), jnp.float32)
    for half in range(2):
        column = lane + half * LANES
        near_edge, near = tile(half)
        far_edge, far = tile(8 + half)
        near = jnp.where(near_edge, near, 0.0)
        far = jnp.where(far_edge, far, 0.0)
        packed[half * R : (half + 1) * R, :] = jnp.where(column >= row, near, far).astype(jnp.bfloat16)
        diagonal = jnp.sum(jnp.where(column == row, far, 0.0), axis=0, keepdims=True)
        tail = jnp.where(place == half, diagonal, tail)
    packed[TILES * R :, :] = tail.astype(jnp.bfloat16)
    leave(slice(0, 2 * R), 0)
    leave(slice(TILES * R, ROWS), 4)
    for part in (1, 2, 3):
        arrive(part)
        for half in range(2):
            index = 2 * part + half
            edge, value = tile(index)
            if part == 2:
                edge = edge | (lane + half * LANES == row)
            packed[index * R : (index + 1) * R, :] = jnp.where(edge, value, 0.0).astype(jnp.bfloat16)
        leave(slice(2 * part * R, 2 * (part + 1) * R), part)
    for copy in leaving:
        copy.wait()


def pack(adjacency, weight):
    hbm = pl.BlockSpec(memory_space=pltpu.HBM)
    return pl.pallas_call(
        pack_kernel,
        in_specs=[hbm, hbm],
        out_specs=hbm,
        out_shape=jax.ShapeDtypeStruct((ROWS, LANES), jnp.bfloat16),
        scratch_shapes=[
            pltpu.VMEM((R, 5 * R), jnp.int32),
            pltpu.VMEM((R, 5 * R), jnp.bfloat16),
            pltpu.VMEM((ROWS, LANES), jnp.bfloat16),
            pltpu.SemaphoreType.DMA((2, 5)),
            pltpu.SemaphoreType.DMA((5,)),
        ],
        compiler_params=pltpu.CompilerParams(vmem_limit_bytes=53 * MIB),
        cost_estimate=pl.CostEstimate(flops=R * 5 * R * 4, bytes_accessed=R * 5 * R * 6 + ROWS * 256, transcendentals=0),
    )(adjacency, weight)


def slot(ref, index):
    begin = index * 2 * R
    return jnp.concatenate([ref[begin : begin + R, :], ref[begin + R : begin + 2 * R, :]], axis=1)


def unpacked(ref):
    row = lax.broadcasted_iota(jnp.int32, (R, R), 0)
    column = lax.broadcasted_iota(jnp.int32, (R, R), 1)
    merged = slot(ref, 0).astype(jnp.float32)
    tail = ref[TILES * R :, :].astype(jnp.float32)
    diagonal = jnp.concatenate([tail[0:1, :], tail[1:2, :]], axis=1)
    first = jnp.where(column >= row, merged, 0.0)
    last = jnp.where(column < row, merged, jnp.where(column == row, diagonal, 0.0))
    return [
        first.astype(jnp.bfloat16),
        slot(ref, 1),
        slot(ref, 2),
        slot(ref, 3),
        last.astype(jnp.bfloat16),
    ]


def block(index):
    return pl.ds(pl.multiple_of(index * R, R), R)


def accumulate(total_ref, left, ref, first_block):
    for offset, right in enumerate(unpacked(ref)):
        where = block(first_block + offset)
        total_ref[:, where] += jnp.dot(left, right, preferred_element_type=jnp.float32)


def near_kernel(sign_ref, own, p0, left_ref, total_ref):
    sign = sign_ref[0]
    for offset, part in enumerate(unpacked(own)):
        left_ref[:, offset * R : (offset + 1) * R] = part
    total_ref[...] = jnp.zeros_like(total_ref)
    for at, ref in ((0, own), (sign, p0)):
        accumulate(total_ref, left_ref[:, block(at + 2)], ref, at + 2)


def square_kernel(sign_ref, left_ref, own, p0, v1, u1, xv1, xu1, before_ref, square_ref, total_ref, work_ref):
    sign = sign_ref[0]
    work_ref[...] = before_ref[...]
    for at, ref in ((-2, u1), (2, v1)):
        accumulate(work_ref, left_ref[:, block(at + 2)], ref, at + 2)

    @pl.when(sign > 0)
    def _():
        accumulate(work_ref, left_ref[:, block(1)], xu1, 1)

    @pl.when(sign < 0)
    def _():
        accumulate(work_ref, left_ref[:, block(3)], xv1, 3)

    square_ref[...] = (work_ref[...] * FIRST_SCALE).astype(jnp.bfloat16)
    total_ref[...] = jnp.zeros_like(total_ref)
    for at, ref in ((0, own), (sign, p0), (-2, u1), (2, v1), (sign - 2, xu1), (sign + 2, xv1)):
        accumulate(total_ref, square_ref[:, block(at + 4)], ref, at + 4)


def piece(ref, index):
    if index in (1, 2, 3):
        return slot(ref, index)
    row = lax.broadcasted_iota(jnp.int32, (R, R), 0)
    column = lax.broadcasted_iota(jnp.int32, (R, R), 1)
    merged = slot(ref, 0).astype(jnp.float32)
    if index == 0:
        return jnp.where(column >= row, merged, 0.0).astype(jnp.bfloat16)
    tail = ref[TILES * R :, :].astype(jnp.float32)
    diagonal = jnp.concatenate([tail[0:1, :], tail[1:2, :]], axis=1)
    return jnp.where(column < row, merged, jnp.where(column == row, diagonal, 0.0)).astype(jnp.bfloat16)


def band_dot(lefts, rows, at):
    places = [place for place in sorted(rows) if abs(at - place) <= 2]
    left = jnp.concatenate([lefts[place][...] for place in places], axis=1)
    right = jnp.concatenate([piece(rows[place], at - place + 2) for place in places], axis=0)
    return jnp.dot(left, right, preferred_element_type=jnp.float32)


def columns_of(ref, place, span):
    return ref.at[:, (place + span) * R : (place + span + 1) * R]


def both_cores(sign_ref, body):
    for sign in (1, -1):
        pl.when(sign_ref[0] == sign)(lambda sign=sign: body(sign))


def forward_kernel(sign_ref, left_ref, own, p0, v1, u1, xv1, xu1, v2, u2, f3, before_ref, cube_ref, rest_ref, sum_ref):
    def body(sign):
        rows = {0: own, sign: p0, -2: u1, 2: v1, sign - 2: xu1, sign + 2: xv1, -4: u2, 4: v2, 6 * sign: f3}
        outer = {place: rows[place] for place in (-4, 4)}
        for at in range(-6, 7):
            value = columns_of(before_ref, at, 6)[...]
            if abs(at) >= 2:
                value = value + band_dot({p: columns_of(left_ref, p, 4) for p in outer}, outer, at)
            if -6 < at * sign < 0:
                columns_of(rest_ref, at * sign, 5)[...] = value
            else:
                columns_of(cube_ref, at, 6)[...] = (value * LAST_SCALE).astype(jnp.bfloat16)
        ready = {place * sign: rows[place * sign] for place in (0, 1, 2, 3, 4, 6)}
        for at in range(-2, 9):
            lefts = {place: columns_of(cube_ref, place, 6) for place in ready}
            columns_of(sum_ref, at * sign, 8)[...] = band_dot(lefts, ready, at * sign)

    both_cores(sign_ref, body)


def edge_kernel(sign_ref, cube_ref, b3, product_ref):
    left = cube_ref[:, block(6 - 6 * sign_ref[0])]
    for index in range(5):
        right = piece(b3, index)
        product_ref[:, index * R : (index + 1) * R] = jnp.dot(left, right, preferred_element_type=jnp.float32)


def last_kernel(
    sign_ref, left_ref, v1, u1, xv1, xu1, v2, u2, xv2, xu2, xf3, edge_ref, cube_ref, rest_ref, sum_ref,
    out_hbm, late_ref, result_ref, semaphores,
):
    def body(sign):
        rows = {-2: u1, 2: v1, sign - 2: xu1, sign + 2: xv1, -4: u2, 4: v2, sign - 4: xu2, sign + 4: xv2}
        rows[-5 * sign] = xf3
        copies = []

        def leave(at, ref, moved=0, span=8):
            place = columns_of(out_hbm, at, 8)
            copy = pltpu.make_async_copy(columns_of(ref, at + moved, span), place, semaphores.at[at + 8])
            copy.start()
            copies.append(copy)

        for at in (2, 8):
            leave(at * sign, sum_ref)
        leave(-8 * sign, edge_ref, 6 * sign, 2)
        third = {-3 * sign: rows[-3 * sign]}
        lefts = {5 * sign: columns_of(cube_ref, 5 * sign, 6)}

        def finish(at):
            value = band_dot(lefts, {place: rows[place] for place in lefts}, at * sign)
            if at <= -4:
                value = value + columns_of(edge_ref, at * sign + 6 * sign, 2)[...]
            if at >= -2:
                value = value + columns_of(sum_ref, at * sign, 8)[...]
            columns_of(result_ref, at * sign, 8)[...] = value
            leave(at * sign, result_ref)

        for at in (3, 4, 5, 6, 7):
            finish(at)
        for at in range(-5, 0):
            value = columns_of(rest_ref, at, 5)[...]
            value = value + band_dot({-3 * sign: columns_of(left_ref, -3 * sign, 4)}, third, at * sign)
            columns_of(late_ref, at, 5)[...] = (value * LAST_SCALE).astype(jnp.bfloat16)
            lefts[at * sign] = columns_of(late_ref, at, 5)
        for at in (1, 0, -1, -2, -3, -4, -5, -6, -7):
            finish(at)
        for copy in copies:
            copy.wait()

    both_cores(sign_ref, body)


def last_call(*arrays):
    return pl.pallas_call(
        last_kernel,
        in_specs=[pl.BlockSpec(memory_space=pltpu.SMEM)] + [pl.BlockSpec(memory_space=pltpu.VMEM)] * (len(arrays) - 1),
        out_specs=pl.BlockSpec(memory_space=pltpu.HBM),
        out_shape=jax.ShapeDtypeStruct((R, 17 * R), jnp.float32),
        scratch_shapes=[
            pltpu.VMEM((R, 5 * R), jnp.bfloat16),
            pltpu.VMEM((R, 17 * R), jnp.float32),
            pltpu.SemaphoreType.DMA((17,)),
        ],
        compiler_params=pltpu.CompilerParams(vmem_limit_bytes=30 * MIB),
        cost_estimate=COST,
    )(*arrays)


COST = pl.CostEstimate(flops=0, bytes_accessed=int(0.1 * MIB), transcendentals=0)


def call(kernel, arrays, shapes, scratch):
    specs = [pl.BlockSpec(memory_space=pltpu.SMEM)]
    specs += [pl.BlockSpec(memory_space=pltpu.VMEM)] * (len(arrays) - 1)
    return pl.pallas_call(
        kernel,
        in_specs=specs,
        out_specs=[pl.BlockSpec(memory_space=pltpu.VMEM)] * len(shapes),
        out_shape=shapes,
        scratch_shapes=scratch,
        compiler_params=pltpu.CompilerParams(vmem_limit_bytes=24 * MIB),
        cost_estimate=COST,
    )(*arrays)


def local(adjacency, weight):
    size = lax.axis_size("blk")
    parity = lax.rem(lax.axis_index("blk"), 2)
    sign = (1 - 2 * parity).astype(jnp.int32).reshape(1)

    def hop(value, steps):
        pairs = []
        for target in range(size):
            ahead = steps if target % 2 == 0 else -steps
            pairs.append(((target + ahead) % size, target))
        return lax.ppermute(value, "blk", pairs)

    def shifted(value, steps):
        return lax.ppermute(value, "blk", [((target + steps) % size, target) for target in range(size)])

    def peer(value):
        return lax.ppermute(value, "blk", [(source, source ^ 1) for source in range(size)])

    tie = lax.optimization_barrier
    f32, bf16 = jnp.float32, jnp.bfloat16
    own = pack(adjacency, weight)
    u1 = shifted(own, -2)
    v1 = shifted(own, 2)
    p0 = peer(own)
    left, total = call(
        near_kernel,
        (sign, own, p0),
        [jax.ShapeDtypeStruct((R, 5 * R), bf16), jax.ShapeDtypeStruct((R, 9 * R), f32)],
        [],
    )
    held, total = tie((own, total))
    f3 = hop(held, 6)
    u2 = shifted(u1, -2)
    v2 = shifted(v1, 2)
    xu1 = peer(u1)
    xv1 = peer(v1)
    f3, total = tie((f3, total))
    square, total = call(
        square_kernel,
        (sign, left, own, p0, v1, u1, xv1, xu1, total),
        [jax.ShapeDtypeStruct((R, 9 * R), bf16), jax.ShapeDtypeStruct((R, 13 * R), f32)],
        [pltpu.VMEM((R, 9 * R), f32)],
    )
    held, total = tie((held, total))
    b3 = hop(held, -6)
    u2, v2, total = tie((u2, v2, total))
    xu2 = peer(u2)
    xv2 = peer(v2)
    xf3 = peer(f3)
    cube, rest, total = call(
        forward_kernel,
        (sign, square, own, p0, v1, u1, xv1, xu1, v2, u2, f3, total),
        [
            jax.ShapeDtypeStruct((R, 13 * R), bf16),
            jax.ShapeDtypeStruct((R, 5 * R), f32),
            jax.ShapeDtypeStruct((R, 17 * R), f32),
        ],
        [],
    )
    (edge,) = call(edge_kernel, (sign, cube, b3), [jax.ShapeDtypeStruct((R, 5 * R), f32)], [])
    return last_call(sign, square, v1, u1, xv1, xu1, v2, u2, xv2, xu2, xf3, edge, cube, rest, total)


def solution(mesh):
    in_specs = (P("blk", None), P("blk", None))
    out_specs = P("blk", None)
    return jax.shard_map(local, mesh=mesh, in_specs=in_specs, out_specs=out_specs, check_vma=False)
```
